256 devices in a mesh: dp: 16 (over y_hi, x, core), feat: 16 (over y_lo, z).
Axes of the slice: x: 4, y: 4 (y_hi: 2, y_lo: 2; y = y_hi * 2 + y_lo), z: 8, core: 2. Of those that a mesh axis runs over, the one named last changes fastest.
Arguments:
- inputs: float32 [8192, 8192], P('dp', 'feat'), may hold values from -6 to 6
- partner_bits: int32 [16, 4], P('feat'), may hold values from 0 to 3, each once within a row
- block_weights: float32 [16, 512, 5, 512], P('feat', 'dp'), may hold values from -0.125 to 0.125
- low_left: float32 [16, 512, 256], P('feat', 'dp'), may hold values from -0.0625 to 0.0625
- low_right: float32 [16, 256, 512], P('feat', 'dp'), may hold values from -0.375 to 0.375
- cotangent: float32 [8192, 8192], P('dp', 'feat'), may hold values from -6 to 6
Outputs:
- outputs: float32 [8192, 8192], P('dp', 'feat')
- input_grad: float32 [8192, 8192], P('dp', 'feat')
- block_grads: float32 [16, 512, 5, 512], P('feat', 'dp')
- left_grads: float32 [16, 512, 256], P('feat', 'dp')
- right_grads: float32 [16, 256, 512], P('feat', 'dp')
The draws below stay inside these ranges and needn't reach their ends.
Inputs may be any that keep to these rules, and one draw needn't show every extreme that they name: `partner_bits`: each row holds every bit number 0 .. 3 once.
All inputs are finite; a program needn't handle non-finite values.
Results may differ from the reference program's by a relative error of at most 0.000086.
Values sent between devices are 32-bit elements; how exact they have to be, the bound alone decides.
A program may use at most 128 MiB of HBM per device.

```python
import jax
import jax.numpy as jnp
from jax import lax

BLOCK = 512
LOWRANK = 256
SECTIONS = 4
WIDTH = 8192
TOKENS = 8192
N_FEAT = 16


def steps_of(own_key, shape, cuts, low, top_value):
    def one(position, shards_of):
        draws = jax.random.uniform(jax.random.fold_in(jax.random.fold_in(own_key, 6), position), (shards_of,), jnp.float32, low / len(cuts), top_value / len(cuts))
        return jnp.repeat(jnp.exp(draws), shape[position] // shards_of).reshape((-1,) + (1,) * (len(shape) - position - 1))

    loudness = one(*cuts[0])
    for cut in cuts[1:]:
        loudness = loudness * one(*cut)
    return loudness


def scatter_about(own_key, dims, scale, limit, split=(), kind=jnp.bfloat16):
    gain = steps_of(own_key, dims, split, -0.22, 0.18) if split else 1.0
    entries = jax.random.normal(own_key, dims, jnp.float32) * scale * gain
    return jnp.minimum(jnp.maximum(entries, -limit), limit).astype(kind)


def setup_inputs(seed: int = 0) -> dict:
    keys = jax.random.split(jax.random.key(seed), 7)
    inputs = scatter_about(keys[0], (TOKENS, WIDTH), 1.0, 6.0, ((0, 16), (1, 16)), jnp.float32)
    partner_bits = jax.vmap(lambda own: jax.random.permutation(own, SECTIONS))(jax.random.split(keys[1], N_FEAT)).reshape((N_FEAT, SECTIONS)).astype(jnp.int32)
    block_weights = scatter_about(keys[2], (N_FEAT, BLOCK, SECTIONS + 1, BLOCK), ((SECTIONS + 1) * BLOCK) ** -0.5, 0.125, ((0, 16), (1, 16)), jnp.float32)
    low_left = scatter_about(keys[3], (N_FEAT, BLOCK, LOWRANK), WIDTH ** -0.5, 0.0625, ((0, 16), (1, 16)), jnp.float32)
    low_right = scatter_about(keys[4], (N_FEAT, LOWRANK, BLOCK), LOWRANK ** -0.5, 0.375, ((0, 16), (1, 16)), jnp.float32)
    cotangent = scatter_about(keys[5], (TOKENS, WIDTH), 1.0, 6.0, ((0, 16), (1, 16)), jnp.float32)
    return {"inputs": inputs, "partner_bits": partner_bits, "block_weights": block_weights, "low_left": low_left, "low_right": low_right, "cotangent": cotangent}


def forward(inputs, block_weights, low_left, low_right, partner_bits):
    highest = lax.Precision.HIGHEST
    blocked = inputs.reshape(TOKENS, N_FEAT, BLOCK)
    owners = jnp.arange(N_FEAT, dtype=jnp.int32)
    others = jnp.bitwise_xor(owners[:, None], jnp.left_shift(jnp.ones_like(partner_bits), partner_bits))
    sources = jnp.concatenate([owners[:, None], others], axis=1).astype(jnp.int32)
    gathered = blocked[:, sources, :]
    sparse = jnp.einsum('tjsi,jiso->tjo', gathered, block_weights, precision=highest)
    codes = jnp.einsum('tji,jir->tr', blocked, low_left, precision=highest)
    lowpart = jnp.einsum('tr,jro->tjo', codes, low_right, precision=highest)
    return (sparse + lowpart).reshape(TOKENS, WIDTH)

def reference(inputs, partner_bits, block_weights, low_left, low_right, cotangent):

    def layer(first, second, third, fourth):
        return forward(first, second, third, fourth, partner_bits)
    outputs, pullback = jax.vjp(layer, inputs, block_weights, low_left, low_right)
    grads = pullback(cotangent)
    scale = 1.0 / jnp.sqrt(jnp.float32(TOKENS))
    return (outputs, grads[0], grads[1] * scale, grads[2] * scale, grads[3] * scale)
```

```python
import functools
import math

import jax
import jax.numpy as jnp
from jax import lax
from jax.experimental import pallas as pl
from jax.experimental.pallas import tpu as pltpu
from jax.sharding import PartitionSpec as P

F32, BF16 = jnp.float32, jnp.bfloat16
N = 512
CHUNKS = 8
ROWS = N // CHUNKS
TILE = 128


def dot(a, b, da, db):
    return lax.dot_general(a, b, (((da,), (db,)), ((), ())), preferred_element_type=F32)


def halves(v):
    high = v.astype(BF16)
    return high, (v - high.astype(F32)).astype(BF16)


def product(a, b, da, db):
    (ah, al), (bh, bl) = a, b
    return dot(ah, bh, da, db) + (dot(ah, bl, da, db) + dot(al, bh, da, db))


def kernel(
    x_ref, g_ref, w_ref, l_ref, r_ref,
    out_ref, dx_ref, bg_ref, lr_out_ref,
    lrg, wg, wh, wl, gh, gl, xr,
    cp, cy, cs, cr, cf,
    pb, r4, r2, rf1, rf2, rf3,
    d, er, e, fr, fs, hr,
    load_sem,
    lr_s, lr_r, w_s, w_r,
    x1_s, x2_s, x8_s, f0_s, f1_s, x_r, x8_r,
    cy_s, cy_r, cs_s, cs_r, cg_s, cg_r, ch_s, ch_r,
    p4_s, p2_s, p1_s, p8_s, r4_r, r2_r, rf1_r, rf2_r, rf3_r,
    d_s, d_r, e_s, e_r, h_s, h_r,
):
    dp, f = lax.axis_index("dp"), lax.axis_index("feat")
    b0, b1, b2, b3 = f % 2, (f // 2) % 2, (f // 4) % 2, f // 8
    z = f % 8
    fx1 = f + 1 - 2 * b0
    fx2 = f + 2 - 4 * b1
    fx3 = fx1 + 2 - 4 * b1
    fx6 = fx2 + 4 - 8 * b2
    fx8 = f + 8 - 16 * b3
    odd = (b0 + b1) % 2 == 1
    even = (b0 + b1) % 2 == 0
    core, x, yh = dp % 2, (dp // 2) % 4, dp // 8
    sib = dp + 1 - 2 * core
    far = dp + 8 - 16 * yh

    def at_x(k):
        return (x + k) % 4

    def dp_x(k):
        return yh * 8 + at_x(k) * 2 + core

    def far_x(k):
        return (1 - yh) * 8 + at_x(k) * 2 + core

    def zs(k):
        return (z + k) % 8

    def copy(src, dst, send, recv, to_dp=None, to_f=None):
        return pltpu.make_async_remote_copy(
            src_ref=src,
            dst_ref=dst,
            send_sem=send,
            recv_sem=recv,
            device_id=(dp if to_dp is None else to_dp, f if to_f is None else to_f),
            device_id_type=pl.DeviceIdType.MESH,
        )

    def arrived(dst, recv):
        copy(dst, dst, recv, recv, to_f=fx1).wait_recv()

    lr = lrg.at[dp]
    loads = [
        pltpu.make_async_copy(l_ref, lr.at[pl.ds(0, 32)], load_sem.at[0]),
        pltpu.make_async_copy(r_ref.at[:, pl.ds(0, 256)], lr.at[pl.ds(32, 16)], load_sem.at[1]),
        pltpu.make_async_copy(r_ref.at[:, pl.ds(256, 256)], lr.at[pl.ds(48, 16)], load_sem.at[2]),
        pltpu.make_async_copy(w_ref, wg.at[dp], load_sem.at[3]),
    ]
    for load in loads:
        load.start()

    barrier = pltpu.get_barrier_semaphore()
    peers = [(dp, b3 * 8 + zs(k)) for k in range(1, 8)] + [(dp, fx8)]
    peers += [(sib, f), (far, f)] + [(dp_x(k), f) for k in range(1, 4)]
    for peer in peers:
        pl.semaphore_signal(barrier, inc=1, device_id=peer, device_id_type=pl.DeviceIdType.MESH)
    pl.semaphore_wait(barrier, len(peers))
    for load in loads:
        load.wait()

    def gather(whole, send, recv):
        def put(slot, index, to):
            return copy(whole.at[slot], whole.at[slot], send.at[index], recv.at[slot], to_dp=to)

        first = [put(dp, 0, far)]
        first += [put(dp, k, dp_x(k)) for k in (1, 3, 2)] + [put(dp, 4, sib)]
        second = [put(far, 4 + k, dp_x(k)) for k in (1, 3, 2)] + [put(far, 8, sib)]
        third = [(dp_x(k), put(dp_x(k), 8 + k, sib)) for k in (1, 3, 2)]
        fourth = [(far_x(k), put(far_x(k), 11 + k, sib)) for k in (1, 3, 2)]

        def start():
            for c in first:
                c.start()

        def relay():
            arrived(whole.at[far], recv.at[far])
            for c in second:
                c.start()

        def pass_on(items):
            for slot, c in items:
                arrived(whole.at[slot], recv.at[slot])
                c.start()

        def finish():
            for y in range(2):
                for k in range(4):
                    slot = y * 8 + k * 2 + 1 - core
                    arrived(whole.at[slot], recv.at[slot])

        def drain():
            for c in first + second + [c for _, c in third + fourth]:
                c.wait_send()

        return start, relay, lambda: pass_on(third), lambda: pass_on(fourth), finish, drain

    lr_start, lr_relay, lr_third, lr_fourth, lr_finish, lr_drain = gather(lrg, lr_s, lr_r)
    w_start, w_relay, w_third, w_fourth, w_finish, w_drain = gather(wg, w_s, w_r)

    def rows(c):
        return pl.ds(c * ROWS, ROWS)

    x_to_1 = [
        copy(x_ref.at[rows(c)], xr.at[0, rows(c)], x1_s.at[c], x_r.at[0, c], to_f=fx1)
        for c in range(CHUNKS)
    ]
    x_to_2 = [
        copy(x_ref.at[rows(c)], xr.at[1, rows(c)], x2_s.at[c], x_r.at[1, c], to_f=fx2)
        for c in range(CHUNKS)
    ]
    x_to_8 = copy(x_ref, xr.at[3], x8_s, x8_r, to_f=fx8)
    fwd_0 = [
        copy(xr.at[0, rows(c)], xr.at[1, rows(c)], f0_s.at[c], x_r.at[1, c], to_f=fx3)
        for c in range(CHUNKS)
    ]
    fwd_1 = [
        copy(xr.at[1, rows(c)], xr.at[2, rows(c)], f1_s.at[c], x_r.at[2, c], to_f=fx6)
        for c in range(CHUNKS)
    ]

    def relay_0(c):
        @pl.when(odd)
        def _():
            arrived(xr.at[0, rows(c)], x_r.at[0, c])
            fwd_0[c].start()

    def relay_1(c):
        arrived(xr.at[1, rows(c)], x_r.at[1, c])
        fwd_1[c].start()

    def tiles(step):
        lax.fori_loop(0, N // TILE, lambda i, _: (step(i), 0)[1], 0)

    def tile(i):
        return pl.ds(pl.multiple_of(i * TILE, TILE), TILE)

    def split_g(i):
        gh[tile(i)], gl[tile(i)] = halves(g_ref[tile(i)])

    def split_w(i):
        for k in range(5):
            block = wg[pl.ds(i * 4, 4), k].reshape(TILE, N)
            wh[k, tile(i)], wl[k, tile(i)] = halves(block)

    def source(k):
        return x_ref if k == 0 else xr.at[k - 1]

    def to_outputs(k):
        def step(i):
            term = product(halves(source(k)[tile(i)]), (wh[k], wl[k]), 1, 0)
            out_ref[tile(i)] = term if k == 0 else out_ref[tile(i)] + term

        tiles(step)

    def to_products(k):
        def step(i):
            term = product((gh[tile(i)], gl[tile(i)]), (wh[k], wl[k]), 1, 1)
            if k == 0:
                dx_ref[tile(i)] = term
            else:
                pb[k - 1, tile(i)] = term

        tiles(step)

    def to_grad(k):
        def step(i):
            part = halves(source(k)[:, tile(i)])
            term = product(part, (gh[...], gl[...]), 0, 0)
            d[k, pl.ds(i * 2, 2)] = term.reshape(2, 2, 32, N)

        tiles(step)

    d_out = [copy(d.at[k, :, 1 - core], er.at[k], d_s.at[k], d_r.at[k], to_dp=sib) for k in range(6)]
    e_out = [
        [
            copy(e.at[k, :, at_x(q)], fr.at[k, q - 1], e_s.at[k, q - 1], e_r.at[k, q - 1], to_dp=dp_x(q))
            for q in (1, 3, 2)
        ]
        for k in range(6)
    ]
    h_out = [copy(fs.at[k, 1 - yh], hr.at[k], h_s.at[k], h_r.at[k], to_dp=far) for k in range(6)]
    scale = 1.0 / math.sqrt(N * 16)

    def sum_1(k):
        d_out[k].start()

    def sum_2(k):
        arrived(er.at[k], d_r.at[k])
        for y in range(2):
            for q in range(4):
                e[k, y, q] = d[k, y * 4 + q, core] + er[k, y * 4 + q]
        for c in e_out[k]:
            c.start()

    def sum_3(k):
        for q in range(3):
            arrived(fr.at[k, q], e_r.at[k, q])
        fs[k] = (e[k, :, x] + fr[k, 0]) + (fr[k, 1] + fr[k, 2])
        h_out[k].start()

    def sum_4(k):
        arrived(hr.at[k], h_r.at[k])
        total = (fs[k, yh] + hr[k]) * scale
        if k < 5:
            bg_ref[k] = total
        else:
            lr_out_ref[...] = total

    cy_out = copy(cp.at[1 - b3], cy, cy_s, cy_r, to_f=fx8)
    cs_out = [
        copy(cp.at[b3, zs(k)], cs.at[k - 1], cs_s.at[k - 1], cs_r.at[k - 1], to_f=b3 * 8 + zs(k))
        for k in range(1, 8)
    ]
    cg_out = [
        copy(cr, cf.at[b3, z], cg_s.at[k - 1], cg_r.at[z], to_f=b3 * 8 + zs(k)) for k in range(1, 8)
    ]
    ch_out = copy(cf.at[b3], cf.at[b3], ch_s, ch_r, to_f=fx8)

    def left_full():
        return lrg[:, 0:32].reshape(N, 256)

    def right_full(half):
        return lrg[:, 32 + 16 * half : 48 + 16 * half].reshape(256, 256)

    def codes_1():
        left = halves(left_full())
        right = [halves(right_full(h)) for h in range(2)]

        def step(i):
            codes = product(halves(x_ref[tile(i)]), left, 1, 0)
            grads = product((gh[tile(i), 0:256], gl[tile(i), 0:256]), right[0], 1, 1)
            grads += product((gh[tile(i), 256:512], gl[tile(i), 256:512]), right[1], 1, 1)
            cp[i // 2, pl.ds((i % 2) * 4, 4), :, 0:256] = codes.reshape(4, 32, 256)
            cp[i // 2, pl.ds((i % 2) * 4, 4), :, 256:512] = grads.reshape(4, 32, 256)

        tiles(step)
        cy_out.start()

    def codes_2():
        arrived(cy, cy_r)
        for q in range(8):
            cp[b3, q] = cp[b3, q] + cy[q]
        for c in cs_out:
            c.start()

    def codes_3():
        for k in range(7):
            arrived(cs.at[k], cs_r.at[k])
        total = cp[b3, z]
        for k in range(7):
            total += cs[k]
        cr[...] = total
        cf[b3, z] = total
        for c in cg_out:
            c.start()

    def codes_4():
        for k in range(1, 8):
            arrived(cf.at[b3, zs(k)], cg_r.at[zs(k)])
        ch_out.start()

    def codes_5():
        arrived(cf.at[1 - b3], ch_r)
        left = halves(left_full())
        right = [halves(right_full(h)) for h in range(2)]

        def codes_of(i):
            return cf[i // 2, pl.ds((i % 2) * 4, 4)].reshape(TILE, N)

        def step(i):
            both = codes_of(i)
            codes, grads = halves(both[:, 0:256]), halves(both[:, 256:512])
            for h in range(2):
                cols = slice(256 * h, 256 * (h + 1))
                out_ref[tile(i), cols] += product(codes, right[h], 1, 0)
            dx_ref[tile(i)] += product(grads, left, 1, 1)

        tiles(step)
        all_codes = cf[...].reshape(N, N)
        grads = halves(all_codes[:, 256:512])

        def left_step(i):
            term = product(halves(x_ref[:, tile(i)]), grads, 0, 0)
            d[5, pl.ds(i * 2, 2), :, :, 0:256] = term.reshape(2, 2, 32, 256)

        tiles(left_step)
        for h in range(2):
            part = halves(all_codes[:, 128 * h : 128 * (h + 1)])
            term = product(part, (gh[...], gl[...]), 0, 0).reshape(4, 2, 16, N)
            d[5, 4 * h : 4 * h + 4, :, 0:16, 256:512] = term[:, :, :, 0:256]
            d[5, 4 * h : 4 * h + 4, :, 16:32, 256:512] = term[:, :, :, 256:512]

    p4_out = [
        copy(pb.at[2, rows(c)], r4.at[rows(c)], p4_s.at[c], r4_r.at[c], to_f=fx6) for c in range(CHUNKS)
    ]
    p2_even = [
        copy(pb.at[1, rows(c)], rf2.at[rows(c)], p2_s.at[c], rf2_r.at[c], to_f=fx2)
        for c in range(CHUNKS)
    ]
    p2_odd = [
        copy(pb.at[1, rows(c)], r2.at[rows(c)], p2_s.at[c], r2_r.at[c], to_f=fx3) for c in range(CHUNKS)
    ]
    p1_out = [
        copy(pb.at[0, rows(c)], rf1.at[rows(c)], p1_s.at[c], rf1_r.at[c], to_f=fx1)
        for c in range(CHUNKS)
    ]
    p8_out = copy(pb.at[3], rf3, p8_s, rf3_r, to_f=fx8)

    def back_2(c):
        arrived(r4.at[rows(c)], r4_r.at[c])
        pb[1, rows(c)] = pb[1, rows(c)] + r4[rows(c)]
        pl.when(even)(p2_even[c].start)
        pl.when(odd)(p2_odd[c].start)

    def back_1(c):
        @pl.when(odd)
        def _():
            arrived(r2.at[rows(c)], r2_r.at[c])
            pb[0, rows(c)] = pb[0, rows(c)] + r2[rows(c)]
            p1_out[c].start()

    def back_0(c):
        arrived(rf1.at[rows(c)], rf1_r.at[c])
        dx_ref[rows(c)] += rf1[rows(c)]

        @pl.when(odd)
        def _():
            arrived(rf2.at[rows(c)], rf2_r.at[c])
            dx_ref[rows(c)] += rf2[rows(c)]

    lr_start()
    for c in range(CHUNKS):
        x_to_1[c].start()

        @pl.when(odd)
        def _():
            x_to_2[c].start()

    w_start()
    x_to_8.start()
    tiles(split_g)
    lr_relay()
    to_grad(0)
    sum_1(0)
    lr_third()
    lr_fourth()
    lr_finish()
    codes_1()
    relay_0(0)
    w_relay()
    relay_0(1)
    relay_0(2)
    codes_2()
    sum_2(0)
    relay_0(3)
    relay_1(0)
    w_third()
    relay_0(4)
    relay_1(1)
    relay_0(5)
    relay_1(2)
    relay_0(6)
    w_fourth()
    relay_1(3)
    relay_0(7)
    w_finish()
    tiles(split_w)
    to_products(3)
    for c in p4_out:
        c.start()
    relay_1(4)
    codes_3()
    to_products(2)
    to_products(1)

    @pl.when(even)
    def _():
        for c in p1_out:
            c.start()

    relay_1(5)
    to_products(4)
    p8_out.start()
    sum_3(0)
    to_products(0)
    to_outputs(0)
    relay_1(6)
    arrived(xr.at[3], x8_r)
    to_grad(4)
    sum_1(4)
    codes_4()
    relay_1(7)
    to_outputs(4)
    sum_2(4)

    @pl.when(even)
    def _():
        for c in range(CHUNKS):
            arrived(xr.at[0, rows(c)], x_r.at[0, c])

    back_2(0)
    to_grad(1)
    sum_1(1)
    back_2(1)
    codes_5()
    sum_1(5)
    back_2(2)
    to_grad(2)
    sum_1(2)
    back_1(0)
    sum_2(1)
    sum_2(5)
    sum_3(4)
    back_2(3)
    to_outputs(1)
    back_1(1)
    to_outputs(2)
    sum_2(2)
    back_2(4)
    for c in range(CHUNKS):
        arrived(xr.at[2, rows(c)], x_r.at[2, c])
    to_grad(3)
    sum_1(3)
    back_1(2)
    back_2(5)
    to_outputs(3)
    sum_2(3)
    for k in (1, 5, 2):
        sum_3(k)
    back_1(3)
    back_2(6)
    arrived(rf3, rf3_r)

    def add_8(i):
        dx_ref[tile(i)] += rf3[tile(i)]

    tiles(add_8)
    sum_3(3)
    back_1(4)
    back_2(7)
    for k in (0, 4, 1, 5, 2):
        sum_4(k)
    back_1(5)
    sum_4(3)
    back_0(0)
    back_1(6)
    back_0(1)
    back_1(7)
    for c in range(2, CHUNKS):
        back_0(c)

    lr_drain()
    w_drain()
    for c in x_to_1 + fwd_1 + p4_out + p1_out + cs_out + cg_out + d_out + h_out:
        c.wait_send()
    for group in e_out:
        for c in group:
            c.wait_send()
    for c in (x_to_8, cy_out, ch_out, p8_out):
        c.wait_send()

    @pl.when(odd)
    def _():
        for c in x_to_2 + fwd_0 + p2_odd:
            c.wait_send()

    @pl.when(even)
    def _():
        for c in p2_even:
            c.wait_send()


def on_device(inputs, partner_bits, block_weights, low_left, low_right, cotangent):
    my_bits = partner_bits[0]
    weights = block_weights[0]
    by_bit = [weights[:, 0]]
    for bit in range(4):
        chosen = weights[:, 1]
        for slot in range(1, 4):
            chosen = jnp.where(my_bits[slot] == bit, weights[:, 1 + slot], chosen)
        by_bit.append(chosen)
    by_bit = jnp.stack(by_bit)

    vmem = pl.BlockSpec(memory_space=pltpu.VMEM)
    hbm = pl.BlockSpec(memory_space=pl.ANY)
    dma = pltpu.SemaphoreType.DMA

    def buf(*shape, dtype=F32):
        return pltpu.VMEM(shape, dtype)

    outputs, input_grad, grads, low = pl.pallas_call(
        kernel,
        out_shape=(
            jax.ShapeDtypeStruct((N, N), F32),
            jax.ShapeDtypeStruct((N, N), F32),
            jax.ShapeDtypeStruct((5, 32, N), F32),
            jax.ShapeDtypeStruct((32, N), F32),
        ),
        in_specs=[vmem, vmem, hbm, hbm, hbm],
        out_specs=(vmem, vmem, vmem, vmem),
        scratch_shapes=[
            buf(16, 64, 256), buf(16, 5, 32, N),
            buf(5, N, N, dtype=BF16), buf(5, N, N, dtype=BF16),
            buf(N, N, dtype=BF16), buf(N, N, dtype=BF16), buf(4, N, N),
            buf(2, 8, 32, N), buf(8, 32, N), buf(7, 32, N), buf(32, N), buf(2, 8, 32, N),
            buf(4, N, N), buf(N, N), buf(N, N), buf(N, N), buf(N, N), buf(N, N),
            buf(6, 8, 2, 32, N), buf(6, 8, 32, N), buf(6, 2, 4, 32, N), buf(6, 3, 2, 32, N),
            buf(6, 2, 32, N), buf(6, 32, N),
            dma((4,)),
            dma((15,)), dma((16,)), dma((15,)), dma((16,)),
            dma((CHUNKS,)), dma((CHUNKS,)), dma, dma((CHUNKS,)), dma((CHUNKS,)), dma((3, CHUNKS)), dma,
            dma, dma, dma((7,)), dma((7,)), dma((7,)), dma((8,)), dma, dma,
            dma((CHUNKS,)), dma((CHUNKS,)), dma((CHUNKS,)), dma,
            dma((CHUNKS,)), dma((CHUNKS,)), dma((CHUNKS,)), dma((CHUNKS,)), dma,
            dma((6,)), dma((6,)), dma((6, 3)), dma((6, 3)), dma((6,)), dma((6,)),
        ],
        compiler_params=pltpu.CompilerParams(
            collective_id=0, has_side_effects=True, vmem_limit_bytes=60 << 20
        ),
    )(inputs, cotangent, by_bit, low_left[0], low_right[0])

    slots = [grads[0]]
    for slot in range(4):
        chosen = grads[1]
        for bit in range(1, 4):
            chosen = jnp.where(my_bits[slot] == bit, grads[1 + bit], chosen)
        slots.append(chosen)
    block_grads = jnp.stack(slots, axis=1)[None]
    left_grads = low[:, 0:256][None]
    right_grads = jnp.concatenate([low[0:16, 256:512], low[16:32, 256:512]], axis=1)[None]
    return outputs, input_grad, block_grads, left_grads, right_grads


def solution(mesh):
    in_specs = (
        P("dp", "feat"),
        P("feat", None),
        P("feat", "dp", None, None),
        P("feat", "dp", None),
        P("feat", "dp", None),
        P("dp", "feat"),
    )
    out_specs = (
        P("dp", "feat"),
        P("dp", "feat"),
        P("feat", "dp", None, None),
        P("feat", "dp", None),
        P("feat", "dp", None),
    )
    return jax.shard_map(on_device, mesh=mesh, in_specs=in_specs, out_specs=out_specs, check_vma=False)
```

```python
import functools
import math

import jax
import jax.numpy as jnp
from jax import lax
from jax.experimental import pallas as pl
from jax.experimental.pallas import tpu as pltpu
from jax.sharding import PartitionSpec as P

F32, BF16 = jnp.float32, jnp.bfloat16
N = 512
CHUNKS = 8
ROWS = N // CHUNKS
TILE = 128


def dot(a, b, da, db):
    return lax.dot_general(a, b, (((da,), (db,)), ((), ())), preferred_element_type=F32)


def halves(v):
    high = v.astype(BF16)
    return high, (v - high.astype(F32)).astype(BF16)


def product(a, b, da, db):
    (ah, al), (bh, bl) = a, b
    return dot(ah, bh, da, db) + (dot(ah, bl, da, db) + dot(al, bh, da, db))


def kernel(
    x_ref, g_ref, bits_ref, w_ref, l_ref, r_ref,
    out_ref, dx_ref, bg_ref, left_ref, right_ref,
    lrg, wg, wh, wl, gh, gl, xr,
    cp, cy, cs, cr, cf,
    pb, r4, r2, rf1, rf2, rf3,
    d, er, e, fr, fs, hr, sums,
    load_sem,
    lr_s, lr_r, w_s, w_r,
    x1_s, x2_s, x8_s, f0_s, f1_s, x_r, x8_r,
    cy_s, cy_r, cs_s, cs_r, cg_s, cg_r, ch_s, ch_r,
    p4_s, p2_s, p1_s, p8_s, r4_r, r2_r, rf1_r, rf2_r, rf3_r,
    d_s, d_r, e_s, e_r, h_s, h_r,
):
    dp, f = lax.axis_index("dp"), lax.axis_index("feat")
    b0, b1, b2, b3 = f % 2, (f // 2) % 2, (f // 4) % 2, f // 8
    z = f % 8
    fx1 = f + 1 - 2 * b0
    fx2 = f + 2 - 4 * b1
    fx3 = fx1 + 2 - 4 * b1
    fx6 = fx2 + 4 - 8 * b2
    fx8 = f + 8 - 16 * b3
    odd = (b0 + b1) % 2 == 1
    even = (b0 + b1) % 2 == 0
    core, x, yh = dp % 2, (dp // 2) % 4, dp // 8
    sib = dp + 1 - 2 * core
    far = dp + 8 - 16 * yh

    def at_x(k):
        return (x + k) % 4

    def dp_x(k):
        return yh * 8 + at_x(k) * 2 + core

    def far_x(k):
        return (1 - yh) * 8 + at_x(k) * 2 + core

    def zs(k):
        return (z + k) % 8

    def copy(src, dst, send, recv, to_dp=None, to_f=None):
        return pltpu.make_async_remote_copy(
            src_ref=src,
            dst_ref=dst,
            send_sem=send,
            recv_sem=recv,
            device_id=(dp if to_dp is None else to_dp, f if to_f is None else to_f),
            device_id_type=pl.DeviceIdType.MESH,
        )

    def arrived(dst, recv):
        copy(dst, dst, recv, recv, to_f=fx1).wait_recv()

    lr = lrg.at[dp]
    loads = [
        pltpu.make_async_copy(l_ref, lr.at[pl.ds(0, 32)], load_sem.at[0]),
        pltpu.make_async_copy(r_ref.at[:, pl.ds(0, 256)], lr.at[pl.ds(32, 16)], load_sem.at[1]),
        pltpu.make_async_copy(r_ref.at[:, pl.ds(256, 256)], lr.at[pl.ds(48, 16)], load_sem.at[2]),
        pltpu.make_async_copy(w_ref, wg.at[dp], load_sem.at[3]),
    ]
    for load in loads:
        load.start()

    barrier = pltpu.get_barrier_semaphore()
    peers = [(dp, b3 * 8 + zs(k)) for k in range(1, 8)] + [(dp, fx8)]
    peers += [(sib, f), (far, f)] + [(dp_x(k), f) for k in range(1, 4)]
    for peer in peers:
        pl.semaphore_signal(barrier, inc=1, device_id=peer, device_id_type=pl.DeviceIdType.MESH)
    pl.semaphore_wait(barrier, len(peers))
    for load in loads:
        load.wait()

    def gather(whole, send, recv):
        def put(slot, index, to):
            return copy(whole.at[slot], whole.at[slot], send.at[index], recv.at[slot], to_dp=to)

        first = [put(dp, 0, far)]
        first += [put(dp, k, dp_x(k)) for k in (1, 3, 2)] + [put(dp, 4, sib)]
        second = [put(far, 4 + k, dp_x(k)) for k in (1, 3, 2)] + [put(far, 8, sib)]
        third = [(dp_x(k), put(dp_x(k), 8 + k, sib)) for k in (1, 3, 2)]
        fourth = [(far_x(k), put(far_x(k), 11 + k, sib)) for k in (1, 3, 2)]

        def start():
            for c in first:
                c.start()

        def relay():
            arrived(whole.at[far], recv.at[far])
            for c in second:
                c.start()

        def pass_on(items):
            for slot, c in items:
                arrived(whole.at[slot], recv.at[slot])
                c.start()

        def finish():
            for y in range(2):
                for k in range(4):
                    slot = y * 8 + k * 2 + 1 - core
                    arrived(whole.at[slot], recv.at[slot])

        def drain():
            for c in first + second + [c for _, c in third + fourth]:
                c.wait_send()

        return start, relay, lambda: pass_on(third), lambda: pass_on(fourth), finish, drain

    lr_start, lr_relay, lr_third, lr_fourth, lr_finish, lr_drain = gather(lrg, lr_s, lr_r)
    w_start, w_relay, w_third, w_fourth, w_finish, w_drain = gather(wg, w_s, w_r)

    def rows(c):
        return pl.ds(c * ROWS, ROWS)

    x_to_1 = [
        copy(x_ref.at[rows(c)], xr.at[0, rows(c)], x1_s.at[c], x_r.at[0, c], to_f=fx1)
        for c in range(CHUNKS)
    ]
    x_to_2 = [
        copy(x_ref.at[rows(c)], xr.at[1, rows(c)], x2_s.at[c], x_r.at[1, c], to_f=fx2)
        for c in range(CHUNKS)
    ]
    x_to_8 = copy(x_ref, xr.at[3], x8_s, x8_r, to_f=fx8)
    fwd_0 = [
        copy(xr.at[0, rows(c)], xr.at[1, rows(c)], f0_s.at[c], x_r.at[1, c], to_f=fx3)
        for c in range(CHUNKS)
    ]
    fwd_1 = [
        copy(xr.at[1, rows(c)], xr.at[2, rows(c)], f1_s.at[c], x_r.at[2, c], to_f=fx6)
        for c in range(CHUNKS)
    ]

    def relay_0(c):
        @pl.when(odd)
        def _():
            arrived(xr.at[0, rows(c)], x_r.at[0, c])
            fwd_0[c].start()

    def relay_1(c):
        arrived(xr.at[1, rows(c)], x_r.at[1, c])
        fwd_1[c].start()

    def tiles(step):
        lax.fori_loop(0, N // TILE, lambda i, _: (step(i), 0)[1], 0)

    def tile(i):
        return pl.ds(pl.multiple_of(i * TILE, TILE), TILE)

    def split_g(i):
        gh[tile(i)], gl[tile(i)] = halves(g_ref[tile(i)])

    bits = [bits_ref[0, slot] for slot in range(4)]
    slots = [0]
    for bit in range(4):
        slot = 1
        for other in range(1, 4):
            slot = jnp.where(bits[other] == bit, other + 1, slot)
        slots.append(slot)

    def split_w(i):
        for k in range(5):
            block = wg[pl.ds(i * 4, 4), slots[k]].reshape(TILE, N)
            wh[k, tile(i)], wl[k, tile(i)] = halves(block)

    def source(k):
        return x_ref if k == 0 else xr.at[k - 1]

    def to_outputs(k):
        def step(i):
            term = product(halves(source(k)[tile(i)]), (wh[k], wl[k]), 1, 0)
            out_ref[tile(i)] = term if k == 0 else out_ref[tile(i)] + term

        tiles(step)

    def to_products(k):
        def step(i):
            term = product((gh[tile(i)], gl[tile(i)]), (wh[k], wl[k]), 1, 1)
            if k == 0:
                dx_ref[tile(i)] = term
            else:
                pb[k - 1, tile(i)] = term

        tiles(step)

    def to_grad(k):
        def step(i):
            part = halves(source(k)[:, tile(i)])
            term = product(part, (gh[...], gl[...]), 0, 0)
            d[k, pl.ds(i * 2, 2)] = term.reshape(2, 2, 32, N)

        tiles(step)

    d_out = [copy(d.at[k, :, 1 - core], er.at[k], d_s.at[k], d_r.at[k], to_dp=sib) for k in range(6)]
    e_out = [
        [
            copy(e.at[k, :, at_x(q)], fr.at[k, q - 1], e_s.at[k, q - 1], e_r.at[k, q - 1], to_dp=dp_x(q))
            for q in (1, 3, 2)
        ]
        for k in range(6)
    ]
    h_out = [copy(fs.at[k, 1 - yh], hr.at[k], h_s.at[k], h_r.at[k], to_dp=far) for k in range(6)]
    scale = 1.0 / math.sqrt(N * 16)

    def sum_1(k):
        d_out[k].start()

    def sum_2(k):
        arrived(er.at[k], d_r.at[k])
        for y in range(2):
            for q in range(4):
                e[k, y, q] = d[k, y * 4 + q, core] + er[k, y * 4 + q]
        for c in e_out[k]:
            c.start()

    def sum_3(k):
        for q in range(3):
            arrived(fr.at[k, q], e_r.at[k, q])
        fs[k] = (e[k, :, x] + fr[k, 0]) + (fr[k, 1] + fr[k, 2])
        h_out[k].start()

    def sum_4(k):
        arrived(hr.at[k], h_r.at[k])
        total = (fs[k, yh] + hr[k]) * scale
        if k == 0:
            bg_ref[0] = total
        elif k < 5:
            sums[k - 1] = total
        else:
            left_ref[...] = total[:, 0:256]
            right_ref[:, 0:256] = total[0:16, 256:512]
            right_ref[:, 256:512] = total[16:32, 256:512]

    def by_slot():
        for slot in range(4):
            bg_ref[1 + slot] = sums[bits[slot]]

    cy_out = copy(cp.at[1 - b3], cy, cy_s, cy_r, to_f=fx8)
    cs_out = [
        copy(cp.at[b3, zs(k)], cs.at[k - 1], cs_s.at[k - 1], cs_r.at[k - 1], to_f=b3 * 8 + zs(k))
        for k in range(1, 8)
    ]
    cg_out = [
        copy(cr, cf.at[b3, z], cg_s.at[k - 1], cg_r.at[z], to_f=b3 * 8 + zs(k)) for k in range(1, 8)
    ]
    ch_out = copy(cf.at[b3], cf.at[b3], ch_s, ch_r, to_f=fx8)

    def left_full():
        return lrg[:, 0:32].reshape(N, 256)

    def right_full(half):
        return lrg[:, 32 + 16 * half : 48 + 16 * half].reshape(256, 256)

    def codes_1():
        left = halves(left_full())
        right = [halves(right_full(h)) for h in range(2)]

        def step(i):
            codes = product(halves(x_ref[tile(i)]), left, 1, 0)
            grads = product((gh[tile(i), 0:256], gl[tile(i), 0:256]), right[0], 1, 1)
            grads += product((gh[tile(i), 256:512], gl[tile(i), 256:512]), right[1], 1, 1)
            cp[i // 2, pl.ds((i % 2) * 4, 4), :, 0:256] = codes.reshape(4, 32, 256)
            cp[i // 2, pl.ds((i % 2) * 4, 4), :, 256:512] = grads.reshape(4, 32, 256)

        tiles(step)
        cy_out.start()

    def codes_2():
        arrived(cy, cy_r)
        for q in range(8):
            cp[b3, q] = cp[b3, q] + cy[q]
        for c in cs_out:
            c.start()

    def codes_3():
        for k in range(7):
            arrived(cs.at[k], cs_r.at[k])
        total = cp[b3, z]
        for k in range(7):
            total += cs[k]
        cr[...] = total
        cf[b3, z] = total
        for c in cg_out:
            c.start()

    def codes_4():
        for k in range(1, 8):
            arrived(cf.at[b3, zs(k)], cg_r.at[zs(k)])
        ch_out.start()

    def codes_5():
        arrived(cf.at[1 - b3], ch_r)
        left = halves(left_full())
        right = [halves(right_full(h)) for h in range(2)]

        def codes_of(i):
            return cf[i // 2, pl.ds((i % 2) * 4, 4)].reshape(TILE, N)

        def step(i):
            both = codes_of(i)
            codes, grads = halves(both[:, 0:256]), halves(both[:, 256:512])
            for h in range(2):
                cols = slice(256 * h, 256 * (h + 1))
                out_ref[tile(i), cols] += product(codes, right[h], 1, 0)
            dx_ref[tile(i)] += product(grads, left, 1, 1)

        tiles(step)
        all_codes = cf[...].reshape(N, N)
        grads = halves(all_codes[:, 256:512])

        def left_step(i):
            term = product(halves(x_ref[:, tile(i)]), grads, 0, 0)
            d[5, pl.ds(i * 2, 2), :, :, 0:256] = term.reshape(2, 2, 32, 256)

        tiles(left_step)
        for h in range(2):
            part = halves(all_codes[:, 128 * h : 128 * (h + 1)])
            term = product(part, (gh[...], gl[...]), 0, 0).reshape(4, 2, 16, N)
            d[5, 4 * h : 4 * h + 4, :, 0:16, 256:512] = term[:, :, :, 0:256]
            d[5, 4 * h : 4 * h + 4, :, 16:32, 256:512] = term[:, :, :, 256:512]

    p4_out = [
        copy(pb.at[2, rows(c)], r4.at[rows(c)], p4_s.at[c], r4_r.at[c], to_f=fx6) for c in range(CHUNKS)
    ]
    p2_even = [
        copy(pb.at[1, rows(c)], rf2.at[rows(c)], p2_s.at[c], rf2_r.at[c], to_f=fx2)
        for c in range(CHUNKS)
    ]
    p2_odd = [
        copy(pb.at[1, rows(c)], r2.at[rows(c)], p2_s.at[c], r2_r.at[c], to_f=fx3) for c in range(CHUNKS)
    ]
    p1_out = [
        copy(pb.at[0, rows(c)], rf1.at[rows(c)], p1_s.at[c], rf1_r.at[c], to_f=fx1)
        for c in range(CHUNKS)
    ]
    p8_out = copy(pb.at[3], rf3, p8_s, rf3_r, to_f=fx8)

    def back_2(c):
        arrived(r4.at[rows(c)], r4_r.at[c])
        pb[1, rows(c)] = pb[1, rows(c)] + r4[rows(c)]
        pl.when(even)(p2_even[c].start)
        pl.when(odd)(p2_odd[c].start)

    def back_1(c):
        @pl.when(odd)
        def _():
            arrived(r2.at[rows(c)], r2_r.at[c])
            pb[0, rows(c)] = pb[0, rows(c)] + r2[rows(c)]
            p1_out[c].start()

    def back_0(c):
        arrived(rf1.at[rows(c)], rf1_r.at[c])
        dx_ref[rows(c)] += rf1[rows(c)]

        @pl.when(odd)
        def _():
            arrived(rf2.at[rows(c)], rf2_r.at[c])
            dx_ref[rows(c)] += rf2[rows(c)]

    def start_x(c):
        x_to_1[c].start()
        pl.when(odd)(x_to_2[c].start)

    lr_start()
    for c in range(4):
        start_x(c)
    w_start()
    tiles(split_g)
    lr_relay()
    lr_third()
    relay_0(0)
    lr_fourth()
    lr_finish()
    w_relay()
    codes_1()
    x_to_8.start()
    relay_0(1)
    to_grad(0)
    sum_1(0)
    relay_0(2)
    relay_1(0)
    relay_0(3)
    relay_1(1)
    w_third()
    codes_2()
    for c in range(4, CHUNKS):
        start_x(c)
    relay_1(2)
    relay_1(3)
    relay_0(4)
    sum_2(0)
    relay_0(5)
    codes_3()
    relay_0(6)
    relay_1(4)
    w_fourth()
    relay_0(7)
    w_finish()
    tiles(split_w)
    to_products(3)
    for c in p4_out:
        c.start()
    relay_1(5)
    to_products(2)
    to_products(1)
    relay_1(6)

    def back_20(c):
        back_2(c)
        pl.when(even)(p1_out[c].start)

    back_20(0)
    relay_1(7)
    back_20(1)
    sum_3(0)
    to_products(4)
    p8_out.start()
    back_20(2)
    arrived(xr.at[3], x8_r)
    to_grad(4)
    sum_1(4)
    back_1(0)
    back_20(3)

    @pl.when(even)
    def _():
        for c in range(CHUNKS):
            arrived(xr.at[0, rows(c)], x_r.at[0, c])

    to_grad(1)
    sum_1(1)
    codes_4()
    back_1(1)
    back_20(4)
    to_grad(2)
    sum_1(2)
    sum_2(4)
    back_1(2)
    to_products(0)
    to_outputs(0)
    back_20(5)
    to_outputs(4)
    sum_2(1)
    back_1(3)
    for c in range(CHUNKS):
        arrived(xr.at[2, rows(c)], x_r.at[2, c])
    to_grad(3)
    sum_1(3)
    back_20(6)
    codes_5()
    sum_1(5)
    sum_2(2)
    sum_3(4)
    back_1(4)
    back_20(7)
    to_outputs(1)
    sum_2(3)
    back_1(5)
    sum_2(5)
    to_outputs(2)
    sum_3(1)
    sum_3(2)
    back_1(6)
    back_0(0)
    to_outputs(3)
    arrived(rf3, rf3_r)

    def add_8(i):
        dx_ref[tile(i)] += rf3[tile(i)]

    tiles(add_8)
    back_1(7)
    back_0(1)
    sum_3(3)
    sum_3(5)
    back_0(2)
    for k in (0, 4, 1, 2):
        sum_4(k)
    back_0(3)
    sum_4(3)
    by_slot()
    sum_4(5)
    for c in range(4, CHUNKS):
        back_0(c)

    lr_drain()
    w_drain()
    for c in x_to_1 + fwd_1 + p4_out + p1_out + cs_out + cg_out + d_out + h_out:
        c.wait_send()
    for group in e_out:
        for c in group:
            c.wait_send()
    for c in (x_to_8, cy_out, ch_out, p8_out):
        c.wait_send()

    @pl.when(odd)
    def _():
        for c in x_to_2 + fwd_0 + p2_odd:
            c.wait_send()

    @pl.when(even)
    def _():
        for c in p2_even:
            c.wait_send()


def on_device(inputs, partner_bits, block_weights, low_left, low_right, cotangent):
    slots = jnp.swapaxes(block_weights[0], 0, 1)
    vmem = pl.BlockSpec(memory_space=pltpu.VMEM)
    smem = pl.BlockSpec(memory_space=pltpu.SMEM)
    hbm = pl.BlockSpec(memory_space=pl.ANY)
    dma = pltpu.SemaphoreType.DMA

    def buf(*shape, dtype=F32):
        return pltpu.VMEM(shape, dtype)

    outputs, input_grad, grads, left_grads, right_grads = pl.pallas_call(
        kernel,
        out_shape=(
            jax.ShapeDtypeStruct((N, N), F32),
            jax.ShapeDtypeStruct((N, N), F32),
            jax.ShapeDtypeStruct((5, 32, N), F32),
            jax.ShapeDtypeStruct((32, 256), F32),
            jax.ShapeDtypeStruct((16, N), F32),
        ),
        in_specs=[vmem, vmem, smem, hbm, hbm, hbm],
        out_specs=(vmem, vmem, vmem, vmem, vmem),
        scratch_shapes=[
            buf(16, 64, 256), buf(16, 5, 32, N),
            buf(5, N, N, dtype=BF16), buf(5, N, N, dtype=BF16),
            buf(N, N, dtype=BF16), buf(N, N, dtype=BF16), buf(4, N, N),
            buf(2, 8, 32, N), buf(8, 32, N), buf(7, 32, N), buf(32, N), buf(2, 8, 32, N),
            buf(4, N, N), buf(N, N), buf(N, N), buf(N, N), buf(N, N), buf(N, N),
            buf(6, 8, 2, 32, N), buf(6, 8, 32, N), buf(6, 2, 4, 32, N), buf(6, 3, 2, 32, N),
            buf(6, 2, 32, N), buf(6, 32, N), buf(4, 32, N),
            dma((4,)),
            dma((15,)), dma((16,)), dma((15,)), dma((16,)),
            dma((CHUNKS,)), dma((CHUNKS,)), dma, dma((CHUNKS,)), dma((CHUNKS,)), dma((3, CHUNKS)), dma,
            dma, dma, dma((7,)), dma((7,)), dma((7,)), dma((8,)), dma, dma,
            dma((CHUNKS,)), dma((CHUNKS,)), dma((CHUNKS,)), dma,
            dma((CHUNKS,)), dma((CHUNKS,)), dma((CHUNKS,)), dma((CHUNKS,)), dma,
            dma((6,)), dma((6,)), dma((6, 3)), dma((6, 3)), dma((6,)), dma((6,)),
        ],
        compiler_params=pltpu.CompilerParams(
            collective_id=0, has_side_effects=True, vmem_limit_bytes=60 << 20
        ),
    )(inputs, cotangent, partner_bits, slots, low_left[0], low_right[0])

    block_grads = jnp.swapaxes(grads, 0, 1)[None]
    return outputs, input_grad, block_grads, left_grads[None], right_grads[None]


def solution(mesh):
    in_specs = (
        P("dp", "feat"),
        P("feat", None),
        P("feat", "dp", None, None),
        P("feat", "dp", None),
        P("feat", "dp", None),
        P("dp", "feat"),
    )
    out_specs = (
        P("dp", "feat"),
        P("dp", "feat"),
        P("feat", "dp", None, None),
        P("feat", "dp", None),
        P("feat", "dp", None),
    )
    return jax.shard_map(on_device, mesh=mesh, in_specs=in_specs, out_specs=out_specs, check_vma=False)
```

```python
import functools
import math

import jax
import jax.numpy as jnp
from jax import lax
from jax.experimental import pallas as pl
from jax.experimental.pallas import tpu as pltpu
from jax.sharding import PartitionSpec as P

F32, BF16 = jnp.float32, jnp.bfloat16
N = 512
CHUNKS = 8
ROWS = N // CHUNKS
TILE = 128


def dot(a, b, da, db):
    return lax.dot_general(a, b, (((da,), (db,)), ((), ())), preferred_element_type=F32)


def halves(v):
    high = v.astype(BF16)
    return high, (v - high.astype(F32)).astype(BF16)


def product(a, b, da, db):
    (ah, al), (bh, bl) = a, b
    return dot(ah, bh, da, db) + (dot(ah, bl, da, db) + dot(al, bh, da, db))


def kernel(
    x_ref, g_ref, bits_ref, w_ref, l_ref, r_ref,
    out_ref, dx_ref, bg_ref, left_ref, right_ref,
    lrg, wg, wh, wl, gh, gl, xr,
    cp, cy, au, ad, cf,
    pb, r4, r2, rf1, rf2, rf3,
    d, er, e, fr, fs, hr, sums,
    load_sem,
    lr_s, lr_r, w_s, w_r,
    x1_s, x2_s, x8_s, f0_s, f1_s, x_r, x8_r,
    cy_s, cy_r, au_s, au_r, ad_s, ad_r, gu_s, gu_r, gd_s, gd_r, ch_s, ch_r,
    p4_s, p2_s, p1_s, p8_s, r4_r, r2_r, rf1_r, rf2_r, rf3_r,
    d_s, d_r, e_s, e_r, h_s, h_r,
):
    dp, f = lax.axis_index("dp"), lax.axis_index("feat")
    b0, b1, b2, b3 = f % 2, (f // 2) % 2, (f // 4) % 2, f // 8
    z = f % 8
    fx1 = f + 1 - 2 * b0
    fx2 = f + 2 - 4 * b1
    fx3 = fx1 + 2 - 4 * b1
    fx6 = fx2 + 4 - 8 * b2
    fx8 = f + 8 - 16 * b3
    odd = (b0 + b1) % 2 == 1
    even = (b0 + b1) % 2 == 0
    core, x, yh = dp % 2, (dp // 2) % 4, dp // 8
    sib = dp + 1 - 2 * core
    far = dp + 8 - 16 * yh

    def at_x(k):
        return (x + k) % 4

    def dp_x(k):
        return yh * 8 + at_x(k) * 2 + core

    def far_x(k):
        return (1 - yh) * 8 + at_x(k) * 2 + core

    def zs(k):
        return (z + k) % 8

    def copy(src, dst, send, recv, to_dp=None, to_f=None):
        return pltpu.make_async_remote_copy(
            src_ref=src,
            dst_ref=dst,
            send_sem=send,
            recv_sem=recv,
            device_id=(dp if to_dp is None else to_dp, f if to_f is None else to_f),
            device_id_type=pl.DeviceIdType.MESH,
        )

    def arrived(dst, recv):
        copy(dst, dst, recv, recv, to_f=fx1).wait_recv()

    lr = lrg.at[dp]
    loads = [
        pltpu.make_async_copy(l_ref, lr.at[pl.ds(0, 32)], load_sem.at[0]),
        pltpu.make_async_copy(r_ref.at[:, pl.ds(0, 256)], lr.at[pl.ds(32, 16)], load_sem.at[1]),
        pltpu.make_async_copy(r_ref.at[:, pl.ds(256, 256)], lr.at[pl.ds(48, 16)], load_sem.at[2]),
        pltpu.make_async_copy(w_ref, wg.at[dp], load_sem.at[3]),
    ]
    for load in loads:
        load.start()

    barrier = pltpu.get_barrier_semaphore()
    peers = [(dp, b3 * 8 + zs(k)) for k in range(1, 8)] + [(dp, fx8)]
    peers += [(sib, f), (far, f)] + [(dp_x(k), f) for k in range(1, 4)]
    for peer in peers:
        pl.semaphore_signal(barrier, inc=1, device_id=peer, device_id_type=pl.DeviceIdType.MESH)
    pl.semaphore_wait(barrier, len(peers))
    for load in loads:
        load.wait()

    def gather(whole, send, recv):
        def put(slot, index, to):
            return copy(whole.at[slot], whole.at[slot], send.at[index], recv.at[slot], to_dp=to)

        first = [put(dp, 0, far)]
        first += [put(dp, k, dp_x(k)) for k in (1, 3, 2)] + [put(dp, 4, sib)]
        second = [put(far, 4 + k, dp_x(k)) for k in (1, 3, 2)] + [put(far, 8, sib)]
        third = [(dp_x(k), put(dp_x(k), 8 + k, sib)) for k in (1, 3, 2)]
        fourth = [(far_x(k), put(far_x(k), 11 + k, sib)) for k in (1, 3, 2)]

        def start():
            for c in first:
                c.start()

        def relay():
            arrived(whole.at[far], recv.at[far])
            for c in second:
                c.start()

        def pass_on(items):
            for slot, c in items:
                arrived(whole.at[slot], recv.at[slot])
                c.start()

        def finish(y):
            for k in range(4):
                slot = y * 8 + k * 2 + 1 - core
                arrived(whole.at[slot], recv.at[slot])

        def drain():
            for c in first + second + [c for _, c in third + fourth]:
                c.wait_send()

        return start, relay, lambda: pass_on(third), lambda: pass_on(fourth), finish, drain

    lr_start, lr_relay, lr_third, lr_fourth, lr_finish, lr_drain = gather(lrg, lr_s, lr_r)
    w_start, w_relay, w_third, w_fourth, w_finish, w_drain = gather(wg, w_s, w_r)

    def rows(c):
        return pl.ds(c * ROWS, ROWS)

    x_to_1 = [
        copy(x_ref.at[rows(c)], xr.at[0, rows(c)], x1_s.at[c], x_r.at[0, c], to_f=fx1)
        for c in range(CHUNKS)
    ]
    x_to_2 = [
        copy(x_ref.at[rows(c)], xr.at[1, rows(c)], x2_s.at[c], x_r.at[1, c], to_f=fx2)
        for c in range(CHUNKS)
    ]
    x_to_8 = copy(x_ref, xr.at[3], x8_s, x8_r, to_f=fx8)
    fwd_0 = [
        copy(xr.at[0, rows(c)], xr.at[1, rows(c)], f0_s.at[c], x_r.at[1, c], to_f=fx3)
        for c in range(CHUNKS)
    ]
    fwd_1 = [
        copy(xr.at[1, rows(c)], xr.at[2, rows(c)], f1_s.at[c], x_r.at[2, c], to_f=fx6)
        for c in range(CHUNKS)
    ]

    def relay_0(c):
        @pl.when(odd)
        def _():
            arrived(xr.at[0, rows(c)], x_r.at[0, c])
            fwd_0[c].start()

    def relay_1(c):
        arrived(xr.at[1, rows(c)], x_r.at[1, c])
        fwd_1[c].start()

    def tiles(step):
        lax.fori_loop(0, N // TILE, lambda i, _: (step(i), 0)[1], 0)

    def tile(i):
        return pl.ds(pl.multiple_of(i * TILE, TILE), TILE)

    def split_g(i):
        gh[tile(i)], gl[tile(i)] = halves(g_ref[tile(i)])

    bits = [bits_ref[0, slot] for slot in range(4)]

    def split_w(half):
        def step(i):
            t = 2 * half + i
            by_slot = [halves(wg[pl.ds(t * 4, 4), slot].reshape(TILE, N)) for slot in range(5)]
            wh[0, tile(t)], wl[0, tile(t)] = by_slot[0]
            for bit in range(4):
                high, low = by_slot[1]
                for other in range(1, 4):
                    here = bits[other] == bit
                    high = jnp.where(here, by_slot[1 + other][0], high)
                    low = jnp.where(here, by_slot[1 + other][1], low)
                wh[1 + bit, tile(t)], wl[1 + bit, tile(t)] = high, low

        lax.fori_loop(0, 2, lambda i, _: (step(i), 0)[1], 0)

    def source(k):
        return x_ref if k == 0 else xr.at[k - 1]

    def to_outputs(k):
        def step(i):
            term = product(halves(source(k)[tile(i)]), (wh[k], wl[k]), 1, 0)
            out_ref[tile(i)] = term if k == 0 else out_ref[tile(i)] + term

        tiles(step)

    def to_products(k, half):
        def step(i):
            mine = pl.ds(pl.multiple_of(half * 256, 256), 256)
            term = product((gh[tile(i)], gl[tile(i)]), (wh[k, mine], wl[k, mine]), 1, 1)
            if k == 0:
                dx_ref[tile(i), mine] = term
            else:
                pb[k - 1, 2 * half, tile(i)] = term[:, 0:128]
                pb[k - 1, 2 * half + 1, tile(i)] = term[:, 128:256]

        tiles(step)

    def to_grad(k):
        def step(i):
            part = halves(source(k)[:, tile(i)])
            term = product(part, (gh[...], gl[...]), 0, 0)
            d[k, pl.ds(i * 2, 2)] = term.reshape(2, 2, 32, N)

        tiles(step)

    d_out = [copy(d.at[k, :, 1 - core], er.at[k], d_s.at[k], d_r.at[k], to_dp=sib) for k in range(6)]
    e_out = [
        [
            copy(e.at[k, :, at_x(q)], fr.at[k, q - 1], e_s.at[k, q - 1], e_r.at[k, q - 1], to_dp=dp_x(q))
            for q in (1, 3, 2)
        ]
        for k in range(6)
    ]
    h_out = [copy(fs.at[k, 1 - yh], hr.at[k], h_s.at[k], h_r.at[k], to_dp=far) for k in range(6)]
    scale = 1.0 / math.sqrt(N * 16)

    def sum_1(k):
        d_out[k].start()

    def sum_2(k):
        arrived(er.at[k], d_r.at[k])
        for y in range(2):
            for q in range(4):
                e[k, y, q] = d[k, y * 4 + q, core] + er[k, y * 4 + q]
        for c in e_out[k]:
            c.start()

    def sum_3(k):
        for q in range(3):
            arrived(fr.at[k, q], e_r.at[k, q])
        fs[k] = (e[k, :, x] + fr[k, 0]) + (fr[k, 1] + fr[k, 2])
        h_out[k].start()

    def sum_4(k):
        arrived(hr.at[k], h_r.at[k])
        total = (fs[k, yh] + hr[k]) * scale
        if k == 0:
            bg_ref[0] = total
        elif k < 5:
            sums[k - 1] = total
        else:
            left_ref[...] = total[:, 0:256]
            right_ref[:, 0:256] = total[0:16, 256:512]
            right_ref[:, 256:512] = total[16:32, 256:512]

    def by_slot():
        for slot in range(4):
            bg_ref[1 + slot] = sums[bits[slot]]

    cy_out = copy(cp.at[1 - b3], cy, cy_s, cy_r, to_f=fx8)
    up, down = b3 * 8 + zs(1), b3 * 8 + zs(7)
    part = [pl.ds(0, 16), pl.ds(16, 16)]

    def both_ways(pick, land, sems, t):
        if t == 0 and land is not None:
            return [
                copy(pick(4).at[part[0]], land[0].at[0, part[0]], sems[0].at[0], sems[1].at[0], to_f=up),
                copy(pick(4).at[part[1]], land[1].at[0, part[1]], sems[2].at[0], sems[3].at[0], to_f=down),
            ]
        if land is not None:
            return [
                copy(pick(4 - t), land[0].at[t], sems[0].at[t], sems[1].at[t], to_f=up),
                copy(pick(4 + t), land[1].at[t], sems[2].at[t], sems[3].at[t], to_f=down),
            ]
        one, two = pick(8 - t), pick(t)
        if t == 3:
            one, two = one.at[part[0]], two.at[part[1]]
        return [
            copy(one, one, sems[0].at[t], sems[1].at[t], to_f=up),
            copy(two, two, sems[2].at[t], sems[3].at[t], to_f=down),
        ]

    cs_out = [
        both_ways(lambda k: cp.at[b3, zs(k)], (au, ad), (au_s, au_r, ad_s, ad_r), t) for t in range(4)
    ]
    cg_out = [both_ways(lambda k: cf.at[b3, zs(k)], None, (gu_s, gu_r, gd_s, gd_r), t) for t in range(4)]
    ch_out = [
        copy(cf.at[b3, zs(k)], cf.at[b3, zs(k)], ch_s.at[k], ch_r.at[zs(k)], to_f=fx8) for k in range(8)
    ]

    def left_full():
        return lrg[:, 0:32].reshape(N, 256)

    def right_full(half):
        return lrg[:, 32 + 16 * half : 48 + 16 * half].reshape(256, 256)

    def codes_1():
        left = halves(left_full())
        right = [halves(right_full(h)) for h in range(2)]

        def step(i):
            codes = product(halves(x_ref[tile(i)]), left, 1, 0)
            grads = product((gh[tile(i), 0:256], gl[tile(i), 0:256]), right[0], 1, 1)
            grads += product((gh[tile(i), 256:512], gl[tile(i), 256:512]), right[1], 1, 1)
            cp[i // 2, pl.ds((i % 2) * 4, 4), :, 0:256] = codes.reshape(4, 32, 256)
            cp[i // 2, pl.ds((i % 2) * 4, 4), :, 256:512] = grads.reshape(4, 32, 256)

        tiles(step)
        cy_out.start()

    def codes_2():
        arrived(cy, cy_r)
        for q in range(8):
            cp[b3, q] = cp[b3, q] + cy[q]
        for c in cs_out[0]:
            c.start()

    def codes_sum(t):
        if t == 1:
            arrived(au.at[0, part[0]], au_r.at[0])
            arrived(ad.at[0, part[1]], ad_r.at[0])
            cp[b3, zs(3), 0:16] = cp[b3, zs(3), 0:16] + au[0, 0:16]
            cp[b3, zs(5), 16:32] = cp[b3, zs(5), 16:32] + ad[0, 16:32]
        else:
            arrived(au.at[t - 1], au_r.at[t - 1])
            arrived(ad.at[t - 1], ad_r.at[t - 1])
            cp[b3, zs(4 - t)] = cp[b3, zs(4 - t)] + au[t - 1]
            cp[b3, zs(4 + t)] = cp[b3, zs(4 + t)] + ad[t - 1]
        for c in cs_out[t]:
            c.start()

    def codes_3():
        arrived(au.at[3], au_r.at[3])
        arrived(ad.at[3], ad_r.at[3])
        cf[b3, z] = (cp[b3, z] + au[3]) + ad[3]
        for c in cg_out[0] + [ch_out[0]]:
            c.start()

    def codes_pass(t):
        arrived(cf.at[b3, zs(8 - t)], gu_r.at[t - 1])
        arrived(cf.at[b3, zs(t)], gd_r.at[t - 1])
        for c in cg_out[t] + [ch_out[8 - t], ch_out[t]]:
            c.start()

    def codes_4():
        arrived(cf.at[b3, zs(4), part[0]], gu_r.at[3])
        arrived(cf.at[b3, zs(4), part[1]], gd_r.at[3])
        ch_out[4].start()

    def codes_5():
        for k in range(8):
            arrived(cf.at[1 - b3, k], ch_r.at[k])
        left = halves(left_full())
        right = [halves(right_full(h)) for h in range(2)]

        def codes_of(i):
            return cf[i // 2, pl.ds((i % 2) * 4, 4)].reshape(TILE, N)

        def step(i):
            both = codes_of(i)
            codes, grads = halves(both[:, 0:256]), halves(both[:, 256:512])
            for h in range(2):
                cols = slice(256 * h, 256 * (h + 1))
                out_ref[tile(i), cols] += product(codes, right[h], 1, 0)
            dx_ref[tile(i)] += product(grads, left, 1, 1)

        tiles(step)
        all_codes = cf[...].reshape(N, N)
        grads = halves(all_codes[:, 256:512])

        def left_step(i):
            term = product(halves(x_ref[:, tile(i)]), grads, 0, 0)
            d[5, pl.ds(i * 2, 2), :, :, 0:256] = term.reshape(2, 2, 32, 256)

        tiles(left_step)
        for h in range(2):
            some = halves(all_codes[:, 128 * h : 128 * (h + 1)])
            term = product(some, (gh[...], gl[...]), 0, 0).reshape(4, 2, 16, N)
            d[5, 4 * h : 4 * h + 4, :, 0:16, 256:512] = term[:, :, :, 0:256]
            d[5, 4 * h : 4 * h + 4, :, 16:32, 256:512] = term[:, :, :, 256:512]

    def block(c):
        return (c // 2 + 2 * yh) % 4

    def chunk(ref, c):
        return ref.at[block(c), pl.ds((c % 2) * 256, 256)]

    def back(bit, ref, send, recv, to):
        return [
            copy(chunk(pb.at[bit], c), chunk(ref, c), send.at[c], recv.at[c], to_f=to)
            for c in range(CHUNKS)
        ]

    p4_out = back(2, r4, p4_s, r4_r, fx6)
    p2_even = back(1, rf2, p2_s, rf2_r, fx2)
    p2_odd = back(1, r2, p2_s, r2_r, fx3)
    p1_out = back(0, rf1, p1_s, rf1_r, fx1)
    p8_out = copy(pb.at[3], rf3, p8_s, rf3_r, to_f=fx8)

    def add_to(bit, ref, c):
        part = (block(c), pl.ds((c % 2) * 256, 256))
        pb[(bit, *part)] = pb[(bit, *part)] + ref[part]

    def add_to_dx(ref, c):
        here = (pl.ds((c % 2) * 256, 256), pl.ds(pl.multiple_of(block(c) * 128, 128), 128))
        dx_ref[here] = dx_ref[here] + ref[block(c), pl.ds((c % 2) * 256, 256)]

    def back_2(c):
        arrived(chunk(r4, c), r4_r.at[c])
        add_to(1, r4, c)
        pl.when(even)(p2_even[c].start)
        pl.when(odd)(p2_odd[c].start)

    def back_1(c):
        @pl.when(odd)
        def _():
            arrived(chunk(r2, c), r2_r.at[c])
            add_to(0, r2, c)
            p1_out[c].start()

    def back_0(c):
        arrived(chunk(rf1, c), rf1_r.at[c])
        add_to_dx(rf1, c)

        @pl.when(odd)
        def _():
            arrived(chunk(rf2, c), rf2_r.at[c])
            add_to_dx(rf2, c)

    def start_x(c):
        x_to_1[c].start()
        pl.when(odd)(x_to_2[c].start)

    def start_p(c):
        p4_out[c].start()

    def add_8():
        arrived(rf3, rf3_r)
        for q in range(4):
            dx_ref[:, 128 * q : 128 * (q + 1)] = dx_ref[:, 128 * q : 128 * (q + 1)] + rf3[q]

    def x0_here():
        @pl.when(even)
        def _():
            for c in range(CHUNKS):
                arrived(xr.at[0, rows(c)], x_r.at[0, c])

    def x2_here():
        for c in range(CHUNKS):
            arrived(xr.at[2, rows(c)], x_r.at[2, c])

    def low_1():
        lr_third()
        lr_fourth()
        lr_finish(0)
        lr_finish(1)
        codes_1()
        x_to_8.start()

    def weights(half):
        w_finish(half)
        split_w(half)

    def x8_grad():
        arrived(xr.at[3], x8_r)
        to_grad(4)
        sum_1(4)

    lr_start()
    start_x(0)
    start_x(1)
    tiles(split_g)
    lr_relay()
    w_start()
    low_1()
    to_grad(0)
    sum_1(0)
    relay_0(0)
    start_x(2)
    relay_0(1)
    start_x(3)
    relay_1(0)
    w_relay()
    codes_2()
    relay_0(2)
    start_x(4)
    relay_1(1)
    w_third()
    weights(yh)
    to_products(3, yh)
    start_p(0); start_p(1)
    to_products(2, yh)
    to_products(1, yh)
    codes_sum(1)
    relay_0(3)
    start_x(5)
    relay_1(2)
    back_2(0)
    start_p(2)
    pl.when(even)(p1_out[0].start)
    sum_2(0)
    codes_sum(2)
    relay_0(4)
    start_x(6)
    relay_1(3)
    back_2(1)
    start_p(3)
    pl.when(even)(p1_out[1].start)
    back_1(0)
    w_fourth()
    weights(1 - yh)
    to_products(3, 1 - yh)
    to_products(2, 1 - yh)
    to_products(1, 1 - yh)
    codes_sum(3)
    relay_0(5)
    start_x(7)
    relay_1(4)
    back_2(2)
    start_p(4)
    pl.when(even)(p1_out[2].start)
    back_1(1)
    x8_grad()
    to_products(4, 0)
    to_products(4, 1)
    p8_out.start()
    codes_3()
    relay_0(6)
    relay_1(5)
    back_2(3)
    start_p(5)
    pl.when(even)(p1_out[3].start)
    back_1(2)
    to_products(0, 0)
    to_products(0, 1)
    sum_2(4)
    codes_pass(1)
    relay_0(7)
    relay_1(6)
    back_2(4)
    start_p(6)
    pl.when(even)(p1_out[4].start)
    back_1(3)
    back_0(0)
    x0_here()
    to_grad(1)
    sum_1(1)
    codes_pass(2)
    relay_1(7)
    back_2(5)
    start_p(7)
    pl.when(even)(p1_out[5].start)
    back_1(4)
    back_0(1)
    to_grad(2)
    sum_1(2)
    sum_3(0)
    codes_pass(3)
    back_2(6)
    pl.when(even)(p1_out[6].start)
    back_1(5)
    back_0(2)
    sum_2(1)
    to_outputs(0)
    codes_4()
    back_2(7)
    pl.when(even)(p1_out[7].start)
    back_1(6)
    back_0(3)
    sum_2(2)
    sum_3(4)
    to_outputs(1)
    back_1(7)
    back_0(4)
    x2_here()
    to_grad(3)
    sum_1(3)
    codes_5()
    sum_1(5)
    sum_3(1)
    back_0(5)
    sum_2(3)
    sum_3(2)
    to_outputs(4)
    sum_2(5)
    back_0(6)
    sum_3(3)
    to_outputs(2)
    add_8()
    sum_3(5)
    back_0(7)
    to_outputs(3)
    sum_4(0)
    sum_4(1)
    sum_4(2)
    sum_4(3)
    sum_4(4)
    sum_4(5)
    by_slot()

    lr_drain()
    w_drain()
    for c in x_to_1 + fwd_1 + p4_out + p1_out + d_out + h_out:
        c.wait_send()
    for group in e_out + cs_out + cg_out + [ch_out]:
        for c in group:
            c.wait_send()
    for c in (x_to_8, cy_out, p8_out):
        c.wait_send()

    @pl.when(odd)
    def _():
        for c in x_to_2 + fwd_0 + p2_odd:
            c.wait_send()

    @pl.when(even)
    def _():
        for c in p2_even:
            c.wait_send()


def on_device(inputs, partner_bits, block_weights, low_left, low_right, cotangent):
    slots = jnp.swapaxes(block_weights[0], 0, 1)
    vmem = pl.BlockSpec(memory_space=pltpu.VMEM)
    smem = pl.BlockSpec(memory_space=pltpu.SMEM)
    hbm = pl.BlockSpec(memory_space=pl.ANY)
    dma = pltpu.SemaphoreType.DMA

    def buf(*shape, dtype=F32):
        return pltpu.VMEM(shape, dtype)

    outputs, input_grad, grads, left_grads, right_grads = pl.pallas_call(
        kernel,
        out_shape=(
            jax.ShapeDtypeStruct((N, N), F32),
            jax.ShapeDtypeStruct((N, N), F32),
            jax.ShapeDtypeStruct((5, 32, N), F32),
            jax.ShapeDtypeStruct((32, 256), F32),
            jax.ShapeDtypeStruct((16, N), F32),
        ),
        in_specs=[vmem, vmem, smem, hbm, hbm, hbm],
        out_specs=(vmem, vmem, vmem, vmem, vmem),
        scratch_shapes=[
            buf(16, 64, 256), buf(16, 5, 32, N),
            buf(5, N, N, dtype=BF16), buf(5, N, N, dtype=BF16),
            buf(N, N, dtype=BF16), buf(N, N, dtype=BF16), buf(4, N, N),
            buf(2, 8, 32, N), buf(8, 32, N), buf(4, 32, N), buf(4, 32, N), buf(2, 8, 32, N),
            buf(4, 4, N, 128), *[buf(4, N, 128)] * 5,
            buf(6, 8, 2, 32, N), buf(6, 8, 32, N), buf(6, 2, 4, 32, N), buf(6, 3, 2, 32, N),
            buf(6, 2, 32, N), buf(6, 32, N), buf(4, 32, N),
            dma((4,)),
            dma((15,)), dma((16,)), dma((15,)), dma((16,)),
            dma((CHUNKS,)), dma((CHUNKS,)), dma, dma((CHUNKS,)), dma((CHUNKS,)), dma((3, CHUNKS)), dma,
            dma, dma, *[dma((4,))] * 8, dma((8,)), dma((8,)),
            dma((CHUNKS,)), dma((CHUNKS,)), dma((CHUNKS,)), dma,
            dma((CHUNKS,)), dma((CHUNKS,)), dma((CHUNKS,)), dma((CHUNKS,)), dma,
            dma((6,)), dma((6,)), dma((6, 3)), dma((6, 3)), dma((6,)), dma((6,)),
        ],
        compiler_params=pltpu.CompilerParams(
            collective_id=0, has_side_effects=True, vmem_limit_bytes=60 << 20
        ),
    )(inputs, cotangent, partner_bits, slots, low_left[0], low_right[0])

    block_grads = jnp.swapaxes(grads, 0, 1)[None]
    return outputs, input_grad, block_grads, left_grads[None], right_grads[None]


def solution(mesh):
    in_specs = (
        P("dp", "feat"),
        P("feat", None),
        P("feat", "dp", None, None),
        P("feat", "dp", None),
        P("feat", "dp", None),
        P("dp", "feat"),
    )
    out_specs = (
        P("dp", "feat"),
        P("dp", "feat"),
        P("feat", "dp", None, None),
        P("feat", "dp", None),
        P("feat", "dp", None),
    )
    return jax.shard_map(on_device, mesh=mesh, in_specs=in_specs, out_specs=out_specs, check_vma=False)
```

```python
import functools
import math

import jax
import jax.numpy as jnp
from jax import lax
from jax.experimental import pallas as pl
from jax.experimental.pallas import tpu as pltpu
from jax.sharding import PartitionSpec as P

F32, BF16 = jnp.float32, jnp.bfloat16
N = 512
CHUNKS = 8
ROWS = N // CHUNKS
TILE = 128


def dot(a, b, da, db):
    return lax.dot_general(a, b, (((da,), (db,)), ((), ())), preferred_element_type=F32)


def halves(v):
    high = v.astype(BF16)
    return high, (v - high.astype(F32)).astype(BF16)


def product(a, b, da, db):
    (ah, al), (bh, bl) = a, b
    return dot(ah, bh, da, db) + (dot(ah, bl, da, db) + dot(al, bh, da, db))


def kernel(
    x_ref, g_ref, bits_ref, w_ref, l_ref, r_ref,
    out_ref, dx_ref, bg_ref, left_ref, right_ref,
    lrg, wg, wh, wl, gh, gl, xr,
    cp, cy, au, ad, cf,
    pb, r4, r2, rf1, rf2, rf3,
    d, er, e, fr, fs, hr, sums,
    load_sem,
    lr_s, lr_r, w_s, w_r,
    x1_s, x2_s, x8_s, f0_s, f1_s, x_r, x8_r,
    cy_s, cy_r, au_s, au_r, ad_s, ad_r, gu_s, gu_r, gd_s, gd_r, ch_s, ch_r,
    p4_s, p2_s, p1_s, p8_s, r4_r, r2_r, rf1_r, rf2_r, rf3_r,
    d_s, d_r, e_s, e_r, h_s, h_r,
):
    dp, f = lax.axis_index("dp"), lax.axis_index("feat")
    b0, b1, b2, b3 = f % 2, (f // 2) % 2, (f // 4) % 2, f // 8
    z = f % 8
    fx1 = f + 1 - 2 * b0
    fx2 = f + 2 - 4 * b1
    fx3 = fx1 + 2 - 4 * b1
    fx6 = fx2 + 4 - 8 * b2
    fx8 = f + 8 - 16 * b3
    odd = (b0 + b1) % 2 == 1
    even = (b0 + b1) % 2 == 0
    core, x, yh = dp % 2, (dp // 2) % 4, dp // 8
    sib = dp + 1 - 2 * core
    far = dp + 8 - 16 * yh

    def at_x(k):
        return (x + k) % 4

    def dp_x(k):
        return yh * 8 + at_x(k) * 2 + core

    def far_x(k):
        return (1 - yh) * 8 + at_x(k) * 2 + core

    def zs(k):
        return (z + k) % 8

    def copy(src, dst, send, recv, to_dp=None, to_f=None):
        return pltpu.make_async_remote_copy(
            src_ref=src,
            dst_ref=dst,
            send_sem=send,
            recv_sem=recv,
            device_id=(dp if to_dp is None else to_dp, f if to_f is None else to_f),
            device_id_type=pl.DeviceIdType.MESH,
        )

    def arrived(dst, recv):
        copy(dst, dst, recv, recv, to_f=fx1).wait_recv()

    lr = lrg.at[dp]
    loads = [
        pltpu.make_async_copy(l_ref, lr.at[pl.ds(0, 32)], load_sem.at[0]),
        pltpu.make_async_copy(r_ref.at[:, pl.ds(0, 256)], lr.at[pl.ds(32, 16)], load_sem.at[1]),
        pltpu.make_async_copy(r_ref.at[:, pl.ds(256, 256)], lr.at[pl.ds(48, 16)], load_sem.at[2]),
        pltpu.make_async_copy(w_ref, wg.at[dp], load_sem.at[3]),
    ]
    for load in loads:
        load.start()

    barrier = pltpu.get_barrier_semaphore()
    peers = [(dp, b3 * 8 + zs(k)) for k in range(1, 8)] + [(dp, fx8)]
    peers += [(sib, f), (far, f)] + [(dp_x(k), f) for k in range(1, 4)]
    for peer in peers:
        pl.semaphore_signal(barrier, inc=1, device_id=peer, device_id_type=pl.DeviceIdType.MESH)
    pl.semaphore_wait(barrier, len(peers))
    for load in loads:
        load.wait()

    def gather(whole, send, recv):
        def put(slot, index, to):
            return copy(whole.at[slot], whole.at[slot], send.at[index], recv.at[slot], to_dp=to)

        first = [put(dp, 0, far)]
        first += [put(dp, k, dp_x(k)) for k in (1, 3, 2)] + [put(dp, 4, sib)]
        second = [put(far, 4 + k, dp_x(k)) for k in (1, 3, 2)] + [put(far, 8, sib)]
        third = [(dp_x(k), put(dp_x(k), 8 + k, sib)) for k in (1, 3, 2)]
        fourth = [(far_x(k), put(far_x(k), 11 + k, sib)) for k in (1, 3, 2)]

        def start():
            for c in first:
                c.start()

        def relay():
            arrived(whole.at[far], recv.at[far])
            for c in second:
                c.start()

        def pass_on(items):
            for slot, c in items:
                arrived(whole.at[slot], recv.at[slot])
                c.start()

        def finish(y):
            for k in range(4):
                slot = y * 8 + k * 2 + 1 - core
                arrived(whole.at[slot], recv.at[slot])

        def drain():
            for c in first + second + [c for _, c in third + fourth]:
                c.wait_send()

        return start, relay, lambda: pass_on(third), lambda: pass_on(fourth), finish, drain

    lr_start, lr_relay, lr_third, lr_fourth, lr_finish, lr_drain = gather(lrg, lr_s, lr_r)
    w_start, w_relay, w_third, w_fourth, w_finish, w_drain = gather(wg, w_s, w_r)

    def rows(c):
        return pl.ds(c * ROWS, ROWS)

    x_to_1 = [
        copy(x_ref.at[rows(c)], xr.at[0, rows(c)], x1_s.at[c], x_r.at[0, c], to_f=fx1)
        for c in range(CHUNKS)
    ]
    x_to_2 = [
        copy(x_ref.at[rows(c)], xr.at[1, rows(c)], x2_s.at[c], x_r.at[1, c], to_f=fx2)
        for c in range(CHUNKS)
    ]
    x_to_8 = copy(x_ref, xr.at[3], x8_s, x8_r, to_f=fx8)
    fwd_0 = [
        copy(xr.at[0, rows(c)], xr.at[1, rows(c)], f0_s.at[c], x_r.at[1, c], to_f=fx3)
        for c in range(CHUNKS)
    ]
    fwd_1 = [
        copy(xr.at[1, rows(c)], xr.at[2, rows(c)], f1_s.at[c], x_r.at[2, c], to_f=fx6)
        for c in range(CHUNKS)
    ]

    def relay_0(c):
        @pl.when(odd)
        def _():
            arrived(xr.at[0, rows(c)], x_r.at[0, c])
            fwd_0[c].start()

    def relay_1(c):
        arrived(xr.at[1, rows(c)], x_r.at[1, c])
        fwd_1[c].start()

    def tiles(step):
        lax.fori_loop(0, N // TILE, lambda i, _: (step(i), 0)[1], 0)

    def tile(i):
        return pl.ds(pl.multiple_of(i * TILE, TILE), TILE)

    def split_g(i):
        gh[tile(i)], gl[tile(i)] = halves(g_ref[tile(i)])

    bits = [bits_ref[0, slot] for slot in range(4)]

    def split_w(half):
        def step(i):
            t = 2 * half + i
            by_slot = [halves(wg[pl.ds(t * 4, 4), slot].reshape(TILE, N)) for slot in range(5)]
            wh[0, tile(t)], wl[0, tile(t)] = by_slot[0]
            for bit in range(4):
                high, low = by_slot[1]
                for other in range(1, 4):
                    here = bits[other] == bit
                    high = jnp.where(here, by_slot[1 + other][0], high)
                    low = jnp.where(here, by_slot[1 + other][1], low)
                wh[1 + bit, tile(t)], wl[1 + bit, tile(t)] = high, low

        lax.fori_loop(0, 2, lambda i, _: (step(i), 0)[1], 0)

    def source(k):
        return x_ref if k == 0 else xr.at[k - 1]

    def to_outputs(k):
        def step(i):
            term = product(halves(source(k)[tile(i)]), (wh[k], wl[k]), 1, 0)
            out_ref[tile(i)] = term if k == 0 else out_ref[tile(i)] + term

        tiles(step)

    def to_products(k, half):
        def step(i):
            mine = pl.ds(pl.multiple_of(half * 256, 256), 256)
            term = product((gh[tile(i)], gl[tile(i)]), (wh[k, mine], wl[k, mine]), 1, 1)
            if k == 0:
                dx_ref[tile(i), mine] = term
            else:
                pb[k - 1, 2 * half, tile(i)] = term[:, 0:128]
                pb[k - 1, 2 * half + 1, tile(i)] = term[:, 128:256]

        tiles(step)

    def to_grad(k):
        def step(i):
            part = halves(source(k)[:, tile(i)])
            term = product(part, (gh[...], gl[...]), 0, 0)
            d[k, pl.ds(i * 2, 2)] = term.reshape(2, 2, 32, N)

        tiles(step)

    d_out = [copy(d.at[k, :, 1 - core], er.at[k], d_s.at[k], d_r.at[k], to_dp=sib) for k in range(6)]
    e_out = [
        [
            copy(e.at[k, :, at_x(q)], fr.at[k, q - 1], e_s.at[k, q - 1], e_r.at[k, q - 1], to_dp=dp_x(q))
            for q in (1, 3, 2)
        ]
        for k in range(6)
    ]
    h_out = [copy(fs.at[k, 1 - yh], hr.at[k], h_s.at[k], h_r.at[k], to_dp=far) for k in range(6)]
    scale = 1.0 / math.sqrt(N * 16)

    def sum_1(k):
        d_out[k].start()

    def sum_2(k):
        arrived(er.at[k], d_r.at[k])
        for y in range(2):
            for q in range(4):
                e[k, y, q] = d[k, y * 4 + q, core] + er[k, y * 4 + q]
        for c in e_out[k]:
            c.start()

    def sum_3(k):
        for q in range(3):
            arrived(fr.at[k, q], e_r.at[k, q])
        fs[k] = (e[k, :, x] + fr[k, 0]) + (fr[k, 1] + fr[k, 2])
        h_out[k].start()

    def sum_4(k):
        arrived(hr.at[k], h_r.at[k])
        total = (fs[k, yh] + hr[k]) * scale
        if k == 0:
            bg_ref[0] = total
        elif k < 5:
            sums[k - 1] = total
        else:
            left_ref[...] = total[:, 0:256]
            right_ref[:, 0:256] = total[0:16, 256:512]
            right_ref[:, 256:512] = total[16:32, 256:512]

    def by_slot():
        for slot in range(4):
            bg_ref[1 + slot] = sums[bits[slot]]

    cy_out = copy(cp.at[1 - b3], cy, cy_s, cy_r, to_f=fx8)
    up, down = b3 * 8 + zs(1), b3 * 8 + zs(7)
    part = [pl.ds(0, 16), pl.ds(16, 16)]

    def both_ways(pick, land, sems, t):
        if t == 0 and land is not None:
            return [
                copy(pick(4).at[part[0]], land[0].at[0, part[0]], sems[0].at[0], sems[1].at[0], to_f=up),
                copy(pick(4).at[part[1]], land[1].at[0, part[1]], sems[2].at[0], sems[3].at[0], to_f=down),
            ]
        if land is not None:
            return [
                copy(pick(4 - t), land[0].at[t], sems[0].at[t], sems[1].at[t], to_f=up),
                copy(pick(4 + t), land[1].at[t], sems[2].at[t], sems[3].at[t], to_f=down),
            ]
        one, two = pick(8 - t), pick(t)
        if t == 3:
            one, two = one.at[part[0]], two.at[part[1]]
        return [
            copy(one, one, sems[0].at[t], sems[1].at[t], to_f=up),
            copy(two, two, sems[2].at[t], sems[3].at[t], to_f=down),
        ]

    cs_out = [
        both_ways(lambda k: cp.at[b3, zs(k)], (au, ad), (au_s, au_r, ad_s, ad_r), t) for t in range(4)
    ]
    cg_out = [both_ways(lambda k: cf.at[b3, zs(k)], None, (gu_s, gu_r, gd_s, gd_r), t) for t in range(4)]
    ch_out = [
        copy(cf.at[b3, zs(k)], cf.at[b3, zs(k)], ch_s.at[k], ch_r.at[zs(k)], to_f=fx8) for k in range(8)
    ]

    def left_full():
        return lrg[:, 0:32].reshape(N, 256)

    def right_full(half):
        return lrg[:, 32 + 16 * half : 48 + 16 * half].reshape(256, 256)

    def codes_1():
        left = halves(left_full())
        right = [halves(right_full(h)) for h in range(2)]

        def step(i):
            codes = product(halves(x_ref[tile(i)]), left, 1, 0)
            grads = product((gh[tile(i), 0:256], gl[tile(i), 0:256]), right[0], 1, 1)
            grads += product((gh[tile(i), 256:512], gl[tile(i), 256:512]), right[1], 1, 1)
            cp[i // 2, pl.ds((i % 2) * 4, 4), :, 0:256] = codes.reshape(4, 32, 256)
            cp[i // 2, pl.ds((i % 2) * 4, 4), :, 256:512] = grads.reshape(4, 32, 256)

        tiles(step)
        cy_out.start()

    def codes_2():
        arrived(cy, cy_r)
        for q in range(8):
            cp[b3, q] = cp[b3, q] + cy[q]
        for c in cs_out[0]:
            c.start()

    def codes_sum(t):
        if t == 1:
            arrived(au.at[0, part[0]], au_r.at[0])
            arrived(ad.at[0, part[1]], ad_r.at[0])
            cp[b3, zs(3), 0:16] = cp[b3, zs(3), 0:16] + au[0, 0:16]
            cp[b3, zs(5), 16:32] = cp[b3, zs(5), 16:32] + ad[0, 16:32]
        else:
            arrived(au.at[t - 1], au_r.at[t - 1])
            arrived(ad.at[t - 1], ad_r.at[t - 1])
            cp[b3, zs(4 - t)] = cp[b3, zs(4 - t)] + au[t - 1]
            cp[b3, zs(4 + t)] = cp[b3, zs(4 + t)] + ad[t - 1]
        for c in cs_out[t]:
            c.start()

    def codes_3():
        arrived(au.at[3], au_r.at[3])
        arrived(ad.at[3], ad_r.at[3])
        cf[b3, z] = (cp[b3, z] + au[3]) + ad[3]
        for c in cg_out[0] + [ch_out[0]]:
            c.start()

    def codes_pass(t):
        arrived(cf.at[b3, zs(8 - t)], gu_r.at[t - 1])
        arrived(cf.at[b3, zs(t)], gd_r.at[t - 1])
        for c in cg_out[t] + [ch_out[8 - t], ch_out[t]]:
            c.start()

    def codes_4():
        arrived(cf.at[b3, zs(4), part[0]], gu_r.at[3])
        arrived(cf.at[b3, zs(4), part[1]], gd_r.at[3])
        ch_out[4].start()

    def codes_5():
        for k in range(8):
            arrived(cf.at[1 - b3, k], ch_r.at[k])
        left = halves(left_full())
        right = [halves(right_full(h)) for h in range(2)]

        def codes_of(i):
            return cf[i // 2, pl.ds((i % 2) * 4, 4)].reshape(TILE, N)

        def step(i):
            both = codes_of(i)
            codes, grads = halves(both[:, 0:256]), halves(both[:, 256:512])
            for h in range(2):
                cols = slice(256 * h, 256 * (h + 1))
                out_ref[tile(i), cols] += product(codes, right[h], 1, 0)
            dx_ref[tile(i)] += product(grads, left, 1, 1)

        tiles(step)
        all_codes = cf[...].reshape(N, N)
        grads = halves(all_codes[:, 256:512])

        def left_step(i):
            term = product(halves(x_ref[:, tile(i)]), grads, 0, 0)
            d[5, pl.ds(i * 2, 2), :, :, 0:256] = term.reshape(2, 2, 32, 256)

        tiles(left_step)
        for h in range(2):
            some = halves(all_codes[:, 128 * h : 128 * (h + 1)])
            term = product(some, (gh[...], gl[...]), 0, 0).reshape(4, 2, 16, N)
            d[5, 4 * h : 4 * h + 4, :, 0:16, 256:512] = term[:, :, :, 0:256]
            d[5, 4 * h : 4 * h + 4, :, 16:32, 256:512] = term[:, :, :, 256:512]

    def block(c):
        return (c // 2 + 2 * yh) % 4

    def chunk(ref, c):
        return ref.at[block(c), pl.ds((c % 2) * 256, 256)]

    def back(bit, ref, send, recv, to):
        return [
            copy(chunk(pb.at[bit], c), chunk(ref, c), send.at[c], recv.at[c], to_f=to)
            for c in range(CHUNKS)
        ]

    p4_out = back(2, r4, p4_s, r4_r, fx6)
    p2_even = back(1, rf2, p2_s, rf2_r, fx2)
    p2_odd = back(1, r2, p2_s, r2_r, fx3)
    p1_out = back(0, rf1, p1_s, rf1_r, fx1)
    p8_out = copy(pb.at[3], rf3, p8_s, rf3_r, to_f=fx8)

    def add_to(bit, ref, c):
        part = (block(c), pl.ds((c % 2) * 256, 256))
        pb[(bit, *part)] = pb[(bit, *part)] + ref[part]

    def add_to_dx(ref, c):
        here = (pl.ds((c % 2) * 256, 256), pl.ds(pl.multiple_of(block(c) * 128, 128), 128))
        dx_ref[here] = dx_ref[here] + ref[block(c), pl.ds((c % 2) * 256, 256)]

    def back_2(c):
        arrived(chunk(r4, c), r4_r.at[c])
        add_to(1, r4, c)
        pl.when(even)(p2_even[c].start)
        pl.when(odd)(p2_odd[c].start)

    def back_1(c):
        @pl.when(odd)
        def _():
            arrived(chunk(r2, c), r2_r.at[c])
            add_to(0, r2, c)
            p1_out[c].start()

    def back_0(c):
        arrived(chunk(rf1, c), rf1_r.at[c])
        add_to_dx(rf1, c)

        @pl.when(odd)
        def _():
            arrived(chunk(rf2, c), rf2_r.at[c])
            add_to_dx(rf2, c)

    def start_x(c):
        x_to_1[c].start()
        pl.when(odd)(x_to_2[c].start)

    def start_p(c):
        p4_out[c].start()

    def add_8():
        arrived(rf3, rf3_r)
        for q in range(4):
            dx_ref[:, 128 * q : 128 * (q + 1)] = dx_ref[:, 128 * q : 128 * (q + 1)] + rf3[q]

    def x0_here():
        @pl.when(even)
        def _():
            for c in range(CHUNKS):
                arrived(xr.at[0, rows(c)], x_r.at[0, c])

    def x2_here():
        for c in range(CHUNKS):
            arrived(xr.at[2, rows(c)], x_r.at[2, c])

    def low_1():
        lr_third()
        lr_fourth()
        lr_finish(0)
        lr_finish(1)
        codes_1()
        x_to_8.start()

    def weights(half):
        w_finish(half)
        split_w(half)

    def x8_grad():
        arrived(xr.at[3], x8_r)
        to_grad(4)
        sum_1(4)

    lr_start()
    start_x(0)
    start_x(1)
    tiles(split_g)
    lr_relay()
    w_start()
    low_1()
    to_grad(0)
    sum_1(0)
    relay_0(0)
    start_x(2)
    relay_0(1)
    start_x(3)
    relay_1(0)
    w_relay()
    codes_2()
    relay_0(2)
    start_x(4)
    relay_1(1)
    w_third()
    weights(yh)
    to_products(3, yh)
    start_p(0); start_p(1)
    to_products(2, yh)
    to_products(1, yh)
    codes_sum(1)
    relay_0(3)
    start_x(5)
    relay_1(2)
    back_2(0)
    start_p(2)
    pl.when(even)(p1_out[0].start)
    sum_2(0)
    codes_sum(2)
    relay_0(4)
    start_x(6)
    relay_1(3)
    back_2(1)
    start_p(3)
    pl.when(even)(p1_out[1].start)
    back_1(0)
    w_fourth()
    weights(1 - yh)
    to_products(3, 1 - yh)
    to_products(2, 1 - yh)
    to_products(1, 1 - yh)
    codes_sum(3)
    relay_0(5)
    start_x(7)
    relay_1(4)
    back_2(2)
    start_p(4)
    pl.when(even)(p1_out[2].start)
    back_1(1)
    x8_grad()
    to_products(4, 0)
    to_products(4, 1)
    p8_out.start()
    codes_3()
    relay_0(6)
    relay_1(5)
    back_2(3)
    start_p(5)
    pl.when(even)(p1_out[3].start)
    back_1(2)
    to_products(0, 0)
    to_products(0, 1)
    sum_2(4)
    codes_pass(1)
    relay_0(7)
    relay_1(6)
    back_2(4)
    start_p(6)
    pl.when(even)(p1_out[4].start)
    back_1(3)
    back_0(0)
    x0_here()
    to_grad(1)
    sum_1(1)
    codes_pass(2)
    relay_1(7)
    back_2(5)
    start_p(7)
    pl.when(even)(p1_out[5].start)
    back_1(4)
    back_0(1)
    to_grad(2)
    sum_1(2)
    sum_3(0)
    codes_pass(3)
    back_2(6)
    pl.when(even)(p1_out[6].start)
    back_1(5)
    back_0(2)
    sum_2(1)
    to_outputs(0)
    codes_4()
    back_2(7)
    pl.when(even)(p1_out[7].start)
    back_1(6)
    back_0(3)
    sum_2(2)
    sum_3(4)
    to_outputs(1)
    back_1(7)
    back_0(4)
    x2_here()
    to_grad(3)
    sum_1(3)
    codes_5()
    sum_1(5)
    sum_3(1)
    back_0(5)
    sum_2(3)
    sum_2(5)
    sum_3(2)
    to_outputs(4)
    back_0(6)
    to_outputs(2)
    to_outputs(3)
    add_8()
    sum_4(0)
    sum_4(4)
    sum_4(1)
    sum_3(3)
    sum_3(5)
    sum_4(2)
    back_0(7)
    sum_4(3)
    by_slot()
    sum_4(5)

    lr_drain()
    w_drain()
    for c in x_to_1 + fwd_1 + p4_out + p1_out + d_out + h_out:
        c.wait_send()
    for group in e_out + cs_out + cg_out + [ch_out]:
        for c in group:
            c.wait_send()
    for c in (x_to_8, cy_out, p8_out):
        c.wait_send()

    @pl.when(odd)
    def _():
        for c in x_to_2 + fwd_0 + p2_odd:
            c.wait_send()

    @pl.when(even)
    def _():
        for c in p2_even:
            c.wait_send()


def on_device(inputs, partner_bits, block_weights, low_left, low_right, cotangent):
    slots = jnp.swapaxes(block_weights[0], 0, 1)
    vmem = pl.BlockSpec(memory_space=pltpu.VMEM)
    smem = pl.BlockSpec(memory_space=pltpu.SMEM)
    hbm = pl.BlockSpec(memory_space=pl.ANY)
    dma = pltpu.SemaphoreType.DMA

    def buf(*shape, dtype=F32):
        return pltpu.VMEM(shape, dtype)

    outputs, input_grad, grads, left_grads, right_grads = pl.pallas_call(
        kernel,
        out_shape=(
            jax.ShapeDtypeStruct((N, N), F32),
            jax.ShapeDtypeStruct((N, N), F32),
            jax.ShapeDtypeStruct((5, 32, N), F32),
            jax.ShapeDtypeStruct((32, 256), F32),
            jax.ShapeDtypeStruct((16, N), F32),
        ),
        in_specs=[vmem, vmem, smem, hbm, hbm, hbm],
        out_specs=(vmem, vmem, vmem, vmem, vmem),
        scratch_shapes=[
            buf(16, 64, 256), buf(16, 5, 32, N),
            buf(5, N, N, dtype=BF16), buf(5, N, N, dtype=BF16),
            buf(N, N, dtype=BF16), buf(N, N, dtype=BF16), buf(4, N, N),
            buf(2, 8, 32, N), buf(8, 32, N), buf(4, 32, N), buf(4, 32, N), buf(2, 8, 32, N),
            buf(4, 4, N, 128), *[buf(4, N, 128)] * 5,
            buf(6, 8, 2, 32, N), buf(6, 8, 32, N), buf(6, 2, 4, 32, N), buf(6, 3, 2, 32, N),
            buf(6, 2, 32, N), buf(6, 32, N), buf(4, 32, N),
            dma((4,)),
            dma((15,)), dma((16,)), dma((15,)), dma((16,)),
            dma((CHUNKS,)), dma((CHUNKS,)), dma, dma((CHUNKS,)), dma((CHUNKS,)), dma((3, CHUNKS)), dma,
            dma, dma, *[dma((4,))] * 8, dma((8,)), dma((8,)),
            dma((CHUNKS,)), dma((CHUNKS,)), dma((CHUNKS,)), dma,
            dma((CHUNKS,)), dma((CHUNKS,)), dma((CHUNKS,)), dma((CHUNKS,)), dma,
            dma((6,)), dma((6,)), dma((6, 3)), dma((6, 3)), dma((6,)), dma((6,)),
        ],
        compiler_params=pltpu.CompilerParams(
            collective_id=0, has_side_effects=True, vmem_limit_bytes=60 << 20
        ),
    )(inputs, cotangent, partner_bits, slots, low_left[0], low_right[0])

    block_grads = jnp.swapaxes(grads, 0, 1)[None]
    return outputs, input_grad, block_grads, left_grads[None], right_grads[None]


def solution(mesh):
    in_specs = (
        P("dp", "feat"),
        P("feat", None),
        P("feat", "dp", None, None),
        P("feat", "dp", None),
        P("feat", "dp", None),
        P("dp", "feat"),
    )
    out_specs = (
        P("dp", "feat"),
        P("dp", "feat"),
        P("feat", "dp", None, None),
        P("feat", "dp", None),
        P("feat", "dp", None),
    )
    return jax.shard_map(on_device, mesh=mesh, in_specs=in_specs, out_specs=out_specs, check_vma=False)
```
